32 devices in a mesh: pipe: 4 (over x, core), expert: 8 (over z, y).
Axes of the slice: x: 2, y: 2, z: 4, core: 2. Of those that a mesh axis runs over, the one named last changes fastest.
Arguments:
- activations: bfloat16 [4, 2, 512, 7168], P('pipe', None, 'expert'), may hold values from -6 to 6
- expert_ids: int32 [4, 2, 512], P('pipe', None, 'expert'), may hold values from 0 to 1, as said below
- gate_values: float32 [4, 2, 512], P('pipe', None, 'expert'), may hold values from 0.5 to 1.5
- norm_gain: bfloat16 [4, 7168], P('pipe'), may hold values from 0.25 to 1.75
- up_weight: bfloat16 [4, 7168, 2048], P('pipe', None, 'expert'), may hold values from -0.0625 to 0.0625
- down_weight: bfloat16 [4, 2048, 7168], P('pipe', 'expert'), may hold values from -0.1875 to 0.1875
Outputs:
- received: bfloat16 [4, 2, 512, 7168], P('pipe', None, 'expert')
The draws below stay inside these ranges and needn't reach their ends.
Inputs may be any that keep to these rules, and one draw needn't show every extreme that they name: `expert_ids`: the 64 tokens of one device in one section and micro-batch (aligned blocks along the last dimension) name no expert more than 48 times; in every section and micro-batch one expert is named exactly 48 times by the tokens of every device.
All inputs are finite; a program needn't handle non-finite values.
Results may differ from the reference program's by a relative error of at most 0.0058.
Values may be sent and summed in bfloat16 or wider, within the bound.
A program may use at most 128 MiB of HBM per device.

```python
import jax
import jax.numpy as jnp
from jax import lax

D = 7168
FF_DEV = 256
TOK = 64
MB = 2
GROUP = 4
FF = 1024
EXPERTS = 2
CAP = 48
SECTIONS = 4
TOKENS = 512
N_EXPERT = 8


def one_block(block_key, hot_expert):
    pool_key, order_key = jax.random.split(block_key)
    others = jnp.arange((EXPERTS - 1) * CAP, dtype=jnp.int32) // CAP
    others = others + (others >= hot_expert).astype(jnp.int32)
    chosen = jax.random.permutation(pool_key, others)[:TOK - CAP]
    merged = jnp.concatenate([jnp.full((CAP,), hot_expert, jnp.int32), chosen])
    return jax.random.permutation(order_key, merged)


def draw_expert_ids(key, part):
    hot_key, block_key = jax.random.split(jax.random.fold_in(key, 17))
    hot_expert = jax.random.randint(hot_key, (SECTIONS * MB,), 0, EXPERTS, dtype=jnp.int32)
    block_keys = jax.random.split(block_key, SECTIONS * MB * N_EXPERT)
    hot_rows = jnp.repeat(hot_expert, N_EXPERT)
    blocks = jax.vmap(one_block)(block_keys, hot_rows)
    return blocks.reshape(SECTIONS, MB, N_EXPERT * TOK).astype(jnp.int32)


def shard_levels(key, dims, cuts, low, largest):
    def one(position, blocks):
        steps = jax.random.uniform(jax.random.fold_in(jax.random.fold_in(key, 6), position), (blocks,), jnp.float32, low / len(cuts), largest / len(cuts))
        return jnp.repeat(jnp.exp(steps), dims[position] // blocks).reshape((-1,) + (1,) * (len(dims) - position - 1))

    factor_of = one(*cuts[0])
    for cut in cuts[1:]:
        factor_of = factor_of * one(*cut)
    return factor_of


def noise(own_key, shape, deviation, bound, cuts=(), kind=jnp.bfloat16):
    values = deviation * jax.random.normal(own_key, shape, jnp.float32)
    if cuts:
        values = values * shard_levels(own_key, shape, cuts, -0.22, 0.18)
    return jnp.clip(values, -bound, bound).astype(kind)


def setup_inputs(seed: int = 0) -> dict:
    key_list = jax.random.split(jax.random.key(seed), 7)
    return {
        "activations": noise(key_list[0], (SECTIONS, MB, TOKENS, D), 1.0, 6.0, ((0, 4), (2, 8))),
        "expert_ids": draw_expert_ids(jax.random.fold_in(key_list[6], 71), 0),
        "gate_values": jnp.clip(0.5 + 1.0 * jax.random.uniform(key_list[2], (SECTIONS, MB, TOKENS), jnp.float32) ** shard_levels(key_list[2], (SECTIONS, MB, TOKENS), ((0, 4), (2, 8)), -0.2, 0.2), 0.5, 1.5),
        "norm_gain": jnp.clip(1.0 + 0.15 * jax.random.normal(key_list[3], (SECTIONS, D), jnp.float32), 0.25, 1.75).astype(jnp.bfloat16),
        "up_weight": noise(key_list[4], (SECTIONS, D, EXPERTS * FF), D ** -0.5, 0.0625, ((0, 4), (2, 8))),
        "down_weight": noise(key_list[5], (SECTIONS, EXPERTS * FF, D), FF ** -0.5, 0.1875, ((0, 4), (1, 8))),
    }


EPSILON = 1e-06

def section_layer(activations, expert_ids, gate_values, norm_gain, up_weight, down_weight):
    widened = activations.astype(jnp.float32)
    scale_inv = lax.rsqrt(lax.optimization_barrier(jnp.mean(widened * widened, axis=-1, keepdims=True)) + EPSILON)
    normed = (widened * scale_inv * norm_gain.astype(jnp.float32)).astype(jnp.bfloat16)
    onehot = (expert_ids[:, None] == jnp.arange(EXPERTS, dtype=jnp.int32)[None, :]).astype(jnp.int32)
    blocked = onehot.reshape(N_EXPERT, TOK, EXPERTS)
    before = jnp.cumsum(blocked, axis=1) - blocked
    ranking = lax.optimization_barrier(jnp.sum(before * blocked, axis=-1)).reshape(TOKENS).astype(jnp.int32)
    source = jnp.arange(TOKENS, dtype=jnp.int32) // TOK
    slot_index = (source * CAP + ranking).astype(jnp.int32)
    buffers = jnp.zeros((EXPERTS, N_EXPERT * CAP, D), jnp.bfloat16).at[expert_ids, slot_index].set(normed)
    up_experts = up_weight.reshape(D, EXPERTS, FF).transpose(1, 0, 2)
    down_experts = down_weight.reshape(EXPERTS, GROUP, FF_DEV, D)
    half_group = GROUP // 2

    def one_expert(packed):
        arriving, up_one, down_one = packed
        hidden = jax.nn.silu(jnp.dot(arriving, up_one, preferred_element_type=jnp.float32)).astype(jnp.bfloat16)
        pieces = hidden.reshape(arriving.shape[0], GROUP, FF_DEV)
        partials = jnp.einsum('rgf,gfd->grd', pieces.astype(jnp.float32), down_one.astype(jnp.float32)).astype(jnp.bfloat16)
        widened_parts = partials.astype(jnp.float32)
        pairs = (widened_parts[:half_group] + widened_parts[half_group:]).astype(jnp.bfloat16)
        pairs = lax.optimization_barrier(pairs)
        return lax.optimization_barrier(jnp.sum(pairs.astype(jnp.float32), axis=0)).astype(jnp.bfloat16)
    results = lax.map(one_expert, (buffers, up_experts, down_experts))
    expert_out = results[expert_ids, slot_index]
    return (widened + gate_values.astype(jnp.float32)[:, None] * expert_out.astype(jnp.float32)).astype(jnp.bfloat16)

def reference(activations, expert_ids, gate_values, norm_gain, up_weight, down_weight):
    section_outputs = []
    for section_index in range(SECTIONS):
        batch_outputs = []
        for batch_index in range(MB):
            batch_outputs.append(section_layer(activations[section_index, batch_index], expert_ids[section_index, batch_index], gate_values[section_index, batch_index], norm_gain[section_index], up_weight[section_index], down_weight[section_index]))
        section_outputs.append(jnp.stack(batch_outputs))
    layer_out = jnp.stack(section_outputs)
    return jnp.roll(layer_out, 1, axis=0)
```

```python
import jax
import jax.numpy as jnp
from jax import lax
from jax.sharding import PartitionSpec as P

LEVELS = 2


EPSILON = 1e-06


def from_behind(value, axis, steps):
    count = lax.axis_size(axis)
    pairs = [(source, (source + steps) % count) for source in range(count)]
    return lax.ppermute(value, axis, pairs)


def one_batch(activations, expert_ids, gate_values, norm_gain, up_local, down_local):
    group_size = 2**LEVELS
    mine = lax.axis_index("expert") // group_size
    widened = activations.astype(jnp.float32)
    scale_inv = lax.rsqrt(jnp.mean(widened * widened, axis=-1, keepdims=True) + EPSILON)
    normed = (widened * scale_inv * norm_gain.astype(jnp.float32)).astype(jnp.bfloat16)
    every = lax.all_gather(normed, "expert", axis=0, tiled=True)
    ids = lax.all_gather(expert_ids, "expert", axis=0, tiled=True)
    hidden = jax.nn.silu(jnp.dot(every, up_local, preferred_element_type=jnp.float32))
    hidden = jnp.where((ids == mine)[:, None], hidden, 0.0).astype(jnp.bfloat16)
    partial_value = jnp.dot(hidden, down_local, preferred_element_type=jnp.float32).astype(jnp.bfloat16)
    expert_out = lax.psum_scatter(partial_value, "expert", scatter_dimension=0, tiled=True)
    return (widened + gate_values[:, None] * expert_out.astype(jnp.float32)).astype(jnp.bfloat16)


def local(activations, expert_ids, gate_values, norm_gain, up_weight, down_weight):
    batches = activations.shape[1]
    received = [
        from_behind(
            one_batch(
                activations[0, batch_index],
                expert_ids[0, batch_index],
                gate_values[0, batch_index],
                norm_gain[0],
                up_weight[0],
                down_weight[0],
            ),
            "pipe",
            1,
        )
        for batch_index in range(batches)
    ]
    return jnp.stack(received)[None]


def solution(mesh):
    placed = (
        P("pipe", None, "expert", None),
        P("pipe", None, "expert"),
        P("pipe", None, "expert"),
        P("pipe", None),
        P("pipe", None, "expert"),
        P("pipe", "expert", None),
    )
    return jax.shard_map(
        local,
        mesh=mesh,
        in_specs=placed,
        out_specs=P("pipe", None, "expert", None),
        check_vma=False,
    )
```

```python
import jax
import jax.numpy as jnp
from jax import lax
from jax.sharding import PartitionSpec as P

LEVELS = 2


EPSILON = 1e-06


def from_behind(value, axis, steps):
    count = lax.axis_size(axis)
    pairs = [(source, (source + steps) % count) for source in range(count)]
    return lax.ppermute(value, axis, pairs)


def exchange(value, groups=None):
    return lax.all_to_all(
        value, "expert", split_axis=0, concat_axis=0, tiled=True, axis_index_groups=groups
    )


def local(activations, expert_ids, gate_values, norm_gain, up_weight, down_weight):
    devices = lax.axis_size("expert")
    group = 2**LEVELS
    experts = devices // group
    groups = [[e * group + j for j in range(group)] for e in range(experts)]
    _, batches, tok, width = activations.shape
    part = width // group
    units = up_weight.shape[2]
    capacity = max(2, 3 * tok // (2 * experts))
    f32, bf16 = jnp.float32, jnp.bfloat16

    up_part = exchange(up_weight[0].reshape(group, part, units), groups)
    down_part = exchange(down_weight[0].reshape(units, group, part).transpose(1, 0, 2), groups)
    down_part = down_part.reshape(group * units, part)

    widened = activations[0].astype(f32)
    scale_inv = lax.rsqrt(jnp.mean(widened * widened, axis=-1, keepdims=True) + EPSILON)
    normed = (widened * scale_inv * norm_gain[0].astype(f32)).astype(bf16)
    onehot = (expert_ids[0][..., None] == jnp.arange(experts, dtype=jnp.int32)).astype(jnp.int32)
    ranking = jnp.sum((jnp.cumsum(onehot, axis=1) - onehot) * onehot, axis=-1)
    slot = expert_ids[0] * capacity + ranking
    place = (slot[..., None] == jnp.arange(experts * capacity, dtype=jnp.int32)).astype(bf16)

    pres = []
    for m in range(batches):
        packed = lax.dot_general(
            place[m], normed[m], (((0,), (0,)), ((), ())), preferred_element_type=f32
        ).astype(bf16)
        packed = packed.reshape(experts, capacity, group, part).transpose(0, 2, 1, 3)
        arriving = exchange(packed.reshape(devices, capacity, part)).reshape(-1, part)
        pres.append(
            jnp.stack([jnp.dot(arriving, up_part[j], preferred_element_type=f32).astype(bf16) for j in range(group)])
        )
    summed = exchange(jnp.concatenate(pres, axis=1), groups).astype(f32)
    hidden = jax.nn.silu(jnp.sum(summed, axis=0)).astype(bf16)
    hidden = exchange(jnp.broadcast_to(hidden[None], (group,) + hidden.shape), groups)
    rows = devices * capacity
    received = []
    for m in range(batches):
        mine = hidden[:, m * rows : (m + 1) * rows]
        mine = jnp.concatenate([mine[j] for j in range(group)], axis=1)
        out = jnp.dot(mine, down_part, preferred_element_type=f32).astype(bf16)
        returned = exchange(out.reshape(devices, capacity, part))
        returned = returned.reshape(experts, group, capacity, part).transpose(0, 2, 1, 3)
        expert_out = jnp.dot(
            place[m], returned.reshape(experts * capacity, width), preferred_element_type=f32
        )
        layer_out = (widened[m] + gate_values[0, m][:, None] * expert_out).astype(bf16)
        received.append(from_behind(layer_out, "pipe", 1))
    return jnp.stack(received)[None]


def solution(mesh):
    placed = (
        P("pipe", None, "expert", None),
        P("pipe", None, "expert"),
        P("pipe", None, "expert"),
        P("pipe", None),
        P("pipe", None, "expert"),
        P("pipe", "expert", None),
    )
    return jax.shard_map(
        local,
        mesh=mesh,
        in_specs=placed,
        out_specs=P("pipe", None, "expert", None),
        check_vma=False,
    )
```

```python
import functools

import jax
import jax.numpy as jnp
from jax import lax
from jax.experimental import pallas as pl
from jax.experimental.pallas import tpu as pltpu
from jax.sharding import PartitionSpec as P

LEVELS = 2


EPSILON = 1e-06
GROUP = 2**LEVELS
MESH = pl.DeviceIdType.MESH
F32, BF16 = jnp.float32, jnp.bfloat16


def remote(source, target, send, recv, **where):
    return pltpu.make_async_remote_copy(
        src_ref=source, dst_ref=target, send_sem=send, recv_sem=recv, device_id=where, device_id_type=MESH
    )


def each(low, high, body):
    def step(index, carry):
        body(index)
        return carry

    lax.fori_loop(low, high, step, 0)


def spread(
    n, pipes, place, act, gain, gate, up, down, up_out, down_out, arrived, act_out, place_out, gate_out,
    packed, wsend, wrecv, dsend, drecv, psend, precv, own,
):
    me, pipe = lax.axis_index("expert"), lax.axis_index("pipe")
    first = (me // GROUP) * GROUP
    g = me - first
    part = packed.shape[-1]
    batches, experts = place.shape[:2]

    barrier = pltpu.get_barrier_semaphore()

    def greet(k):
        pl.semaphore_signal(barrier, inc=1, device_id={"expert": (me + k) % n}, device_id_type=MESH)

    each(1, n, greet)
    pl.semaphore_signal(barrier, inc=1, device_id={"pipe": (pipe + pipes - 1) % pipes}, device_id_type=MESH)
    pl.semaphore_wait(barrier, n)

    def columns(j):
        return pl.ds(pl.multiple_of(j * part, 128), part)

    waits = []
    for k in range(1, GROUP):
        j = (g + k) % GROUP
        copy = remote(up.at[j], up_out.at[g], wsend.at[0, k], wrecv.at[0, k], expert=first + j)
        copy.start()
        waits.append(copy)
    for i, (source, target) in enumerate(((act, act_out), (place, place_out), (gate, gate_out))):
        copy = remote(source, target, psend.at[i], precv.at[i], pipe=(pipe + 1) % pipes)
        copy.start()
        waits.append(copy)
    locals_ = [
        pltpu.make_async_copy(up.at[g], up_out.at[g], own.at[0]),
        pltpu.make_async_copy(down.at[:, columns(g)], down_out.at[g], own.at[1]),
    ]
    for copy in locals_:
        copy.start()

    for m in range(batches):
        wide = act[m].astype(F32)
        scale = lax.rsqrt(jnp.mean(wide * wide, axis=-1, keepdims=True) + EPSILON)
        normed = (wide * scale * gain[...].astype(F32)).astype(BF16)
        for e in range(experts):
            for j in range(GROUP):
                packed[m, e * GROUP + j] = jnp.dot(
                    place[m, e], normed[:, j * part : (j + 1) * part], preferred_element_type=F32
                ).astype(BF16)

        def send(k, m=m):
            d = (me + k) % n
            remote(packed.at[m, d], arrived.at[m, me], dsend.at[m, k], drecv.at[m, k], expert=d).start()

        each(1, n, send)
        copy = pltpu.make_async_copy(packed.at[m, me], arrived.at[m, me], own.at[2 + m])
        copy.start()
        locals_.append(copy)

    for k in range(1, GROUP):
        j = (g + k) % GROUP
        copy = remote(
            down.at[:, columns(j)], down_out.at[g], wsend.at[1, k], wrecv.at[1, k], expert=first + j
        )
        copy.start()
        waits.append(copy)

    for copy in locals_:
        copy.wait()
    for copy in waits:
        copy.wait()
    for m in range(batches):

        def finish(k, m=m):
            d = (me + k) % n
            remote(packed.at[m, d], arrived.at[m, me], dsend.at[m, k], drecv.at[m, k], expert=d).wait()

        each(1, n, finish)


def experts_kernel(
    n, pipes, x, up, down, ret, pres, sums, own_pre, hidden, out, ssend, srecv, hsend, hrecv, rsend, rrecv,
):
    me, pipe = lax.axis_index("expert"), lax.axis_index("pipe")
    group_index = me // GROUP
    first = group_index * GROUP
    g = me - first
    batches, capacity = ret.shape[0], ret.shape[2]
    units = up.shape[2]
    ahead, behind = (pipe + 1) % pipes, (pipe + pipes - 1) % pipes

    barrier = pltpu.get_barrier_semaphore()
    for k in range(1, GROUP):
        pl.semaphore_signal(
            barrier, inc=1, device_id={"expert": first + (g + k) % GROUP}, device_id_type=MESH
        )

    def greet(k):
        pl.semaphore_signal(barrier, inc=1, device_id={"pipe": behind, "expert": k}, device_id_type=MESH)

    each(0, n, greet)
    pl.semaphore_wait(barrier, n + GROUP - 1)

    copies = []
    for k in range(1, GROUP):
        j = (g + k) % GROUP
        pres[k] = jnp.dot(x[...], up[j], preferred_element_type=F32).astype(BF16)
        copy = remote(pres.at[k], sums.at[k], ssend.at[k], srecv.at[k], expert=first + j)
        copy.start()
        copies.append(copy)
    own_pre[...] = jnp.dot(x[...], up[g], preferred_element_type=F32)
    for copy in copies:
        copy.wait()
    total = own_pre[...]
    for k in range(1, GROUP):
        total = total + sums[k].astype(F32)
    mine = pl.ds(pl.multiple_of(g * units, 128), units)
    hidden[:, mine] = jax.nn.silu(total).astype(BF16)
    copies = []
    for k in range(1, GROUP):
        copy = remote(
            hidden.at[:, mine], hidden.at[:, mine], hsend.at[k], hrecv.at[k], expert=first + (g + k) % GROUP
        )
        copy.start()
        copies.append(copy)
    for copy in copies:
        copy.wait()

    blocks = n // GROUP
    tall = GROUP * capacity

    def block(index):
        m = index // blocks
        owner = (group_index + 1 + index) % blocks
        rows = pl.ds(pl.multiple_of((m * blocks + owner) * tall, 16), tall)
        out[rows, :] = jnp.dot(hidden[rows, :], down[...], preferred_element_type=F32).astype(BF16)
        for j in range(GROUP):
            target = owner * GROUP + j
            give(m, target).start()

    def give(m, target):
        rows = pl.ds(pl.multiple_of((m * n + target) * capacity, 16), capacity)
        return remote(
            out.at[rows, :], ret.at[m, me], rsend.at[m, target], rrecv.at[m, me], pipe=ahead, expert=target
        )

    each(0, batches * blocks, block)

    def finish(index):
        m, source = index // n, index % n
        give(m, source).wait_send()
        rows = pl.ds(pl.multiple_of(index * capacity, 16), capacity)
        remote(
            out.at[rows, :], ret.at[m, source], rsend.at[m, source], rrecv.at[m, source],
            pipe=ahead, expert=source,
        ).wait_recv()

    each(0, batches * n, finish)


def local(pipes, activations, expert_ids, gate_values, norm_gain, up_weight, down_weight):
    n = lax.axis_size("expert")
    experts = n // GROUP
    _, batches, tok, width = activations.shape
    part = width // GROUP
    units = up_weight.shape[2]
    capacity = max(2, 3 * tok // (2 * experts))
    capacity = (capacity + 15) // 16 * 16
    rows = batches * n * capacity

    onehot = (expert_ids[0][..., None] == jnp.arange(experts, dtype=jnp.int32)).astype(jnp.int32)
    ranking = jnp.sum((jnp.cumsum(onehot, axis=1) - onehot) * onehot, axis=-1)
    slot = expert_ids[0] * capacity + ranking
    slots = jnp.arange(experts * capacity, dtype=jnp.int32).reshape(1, experts, capacity, 1)
    place = (slot[:, None, None, :] == slots).astype(BF16)

    vmem, far = pl.BlockSpec(memory_space=pltpu.VMEM), pl.BlockSpec(memory_space=pl.ANY)
    shape, sem = jax.ShapeDtypeStruct, pltpu.SemaphoreType.DMA
    up_part, down_part, arrived, act_prev, place_prev, gate_prev = pl.pallas_call(
        functools.partial(spread, n, pipes),
        out_shape=(
            shape((GROUP, part, units), BF16),
            shape((GROUP, units, part), BF16),
            shape((batches, n, capacity, part), BF16),
            shape((batches, tok, width), BF16),
            shape(place.shape, BF16),
            shape((batches, tok), F32),
        ),
        in_specs=[vmem] * 4 + [far] * 2,
        out_specs=(far,) * 6,
        scratch_shapes=[
            pltpu.VMEM((batches, n, capacity, part), BF16),
            sem((2, GROUP)),
            sem((2, GROUP)),
            sem((batches, n)),
            sem((batches, n)),
            sem((3,)),
            sem((3,)),
            sem((2 + batches,)),
        ],
        compiler_params=pltpu.CompilerParams(
            collective_id=0, has_side_effects=True, vmem_limit_bytes=40 * 2**20
        ),
    )(
        place,
        activations[0],
        norm_gain,
        gate_values[0],
        up_weight[0].reshape(GROUP, part, units),
        down_weight[0],
    )

    returned = pl.pallas_call(
        functools.partial(experts_kernel, n, pipes),
        out_shape=shape((batches, n, capacity, part), BF16),
        in_specs=[vmem] * 3,
        out_specs=far,
        scratch_shapes=[
            pltpu.VMEM((GROUP, rows, units), BF16),
            pltpu.VMEM((GROUP, rows, units), BF16),
            pltpu.VMEM((rows, units), F32),
            pltpu.VMEM((rows, GROUP * units), BF16),
            pltpu.VMEM((rows, part), BF16),
            sem((GROUP,)),
            sem((GROUP,)),
            sem((GROUP,)),
            sem((GROUP,)),
            sem((batches, n)),
            sem((batches, n)),
        ],
        compiler_params=pltpu.CompilerParams(
            collective_id=1, has_side_effects=True, vmem_limit_bytes=60 * 2**20
        ),
    )(arrived.reshape(rows, part), up_part, down_part.reshape(GROUP * units, part))

    returned = returned.reshape(batches, experts, GROUP, capacity, part)
    finished = []
    for m in range(batches):
        table = returned[m].transpose(0, 2, 1, 3).reshape(experts * capacity, width)
        expert_out = lax.dot_general(
            place_prev[m].reshape(experts * capacity, tok),
            table,
            (((0,), (0,)), ((), ())),
            preferred_element_type=F32,
        )
        finished.append((act_prev[m].astype(F32) + gate_prev[m][:, None] * expert_out).astype(BF16))
    return jnp.stack(finished)[None]


def solution(mesh):
    placed = (
        P("pipe", None, "expert", None),
        P("pipe", None, "expert"),
        P("pipe", None, "expert"),
        P("pipe", None),
        P("pipe", None, "expert"),
        P("pipe", "expert", None),
    )
    return jax.shard_map(
        functools.partial(local, mesh.shape["pipe"]),
        mesh=mesh,
        in_specs=placed,
        out_specs=P("pipe", None, "expert", None),
        check_vma=False,
    )
```

```python
import functools

import jax
import jax.numpy as jnp
from jax import lax
from jax.experimental import pallas as pl
from jax.experimental.pallas import tpu as pltpu
from jax.sharding import PartitionSpec as P

LEVELS = 2


EPSILON = 1e-06
GROUP = 2**LEVELS
MESH = pl.DeviceIdType.MESH
F32, BF16 = jnp.float32, jnp.bfloat16


def remote(source, target, send, recv, **where):
    return pltpu.make_async_remote_copy(
        src_ref=source, dst_ref=target, send_sem=send, recv_sem=recv, device_id=where, device_id_type=MESH
    )


def each(low, high, body):
    def step(index, carry):
        body(index)
        return carry

    lax.fori_loop(low, high, step, 0)


def layer_kernel(
    n, pipes, place, act, gain, gate, up, down, ret, act_out, place_out, gate_out,
    packed, x, up_all, down_all, pres, sums, own_pre, hidden, out,
    usend, urecv, dsend, drecv, psend, precv, xsend, xrecv, ssend, srecv, hsend, hrecv, rsend, rrecv, own,
):
    me, pipe = lax.axis_index("expert"), lax.axis_index("pipe")
    group_index = me // GROUP
    first = group_index * GROUP
    g = me - first
    batches, experts, capacity = place.shape[:3]
    part, units = up.shape[1:]
    ahead, behind = (pipe + 1) % pipes, (pipe + pipes - 1) % pipes
    blocks = n // GROUP
    tall = GROUP * capacity

    barrier = pltpu.get_barrier_semaphore()

    def greet(k):
        pl.semaphore_signal(barrier, inc=1, device_id={"expert": (me + k) % n}, device_id_type=MESH)

    def greet_behind(k):
        pl.semaphore_signal(barrier, inc=1, device_id={"pipe": behind, "expert": k}, device_id_type=MESH)

    each(1, n, greet)
    each(0, n, greet_behind)
    pl.semaphore_wait(barrier, 2 * n - 1)

    def columns(j):
        return pl.ds(pl.multiple_of(j * part, 128), part)

    def share(j):
        return pl.ds(pl.multiple_of(j * units, 128), units)

    def rows_of(d):
        return pl.ds(pl.multiple_of(d * capacity, 16), capacity)

    peers = [(k, (g + k) % GROUP) for k in range(1, GROUP)]
    ups = [remote(up.at[j], up_all.at[g], usend.at[k], urecv.at[k], expert=first + j) for k, j in peers]
    downs = [
        remote(
            down.at[:, columns(j)], down_all.at[share(g), :], dsend.at[k], drecv.at[k], expert=first + j
        )
        for k, j in peers
    ]
    shifts = [
        remote(source, target, psend.at[i], precv.at[i], pipe=ahead)
        for i, (source, target) in enumerate(((act, act_out), (place, place_out), (gate, gate_out)))
    ]

    def dispatch(m, k):
        d = (me + k) % n
        return remote(packed.at[m, d], x.at[m, rows_of(me), :], xsend.at[m, k], xrecv.at[m, k], expert=d)

    for copy in ups:
        copy.start()
    own_up = pltpu.make_async_copy(up.at[g], up_all.at[g], own.at[0])
    own_down = pltpu.make_async_copy(down.at[:, columns(g)], down_all.at[share(g), :], own.at[1])
    own_up.start()
    own_down.start()
    own_rows = []
    for m in range(batches):
        wide = act[m].astype(F32)
        scale = lax.rsqrt(jnp.mean(wide * wide, axis=-1, keepdims=True) + EPSILON)
        normed = (wide * scale * gain[...].astype(F32)).astype(BF16)
        for e in range(experts):
            for j in range(GROUP):
                packed[m, e * GROUP + j] = jnp.dot(
                    place[m, e], normed[:, j * part : (j + 1) * part], preferred_element_type=F32
                ).astype(BF16)
        each(1, n, lambda k, m=m: dispatch(m, k).start())
        copy = pltpu.make_async_copy(packed.at[m, me], x.at[m, rows_of(me), :], own.at[2 + m])
        copy.start()
        own_rows.append(copy)
    for copy in shifts:
        copy.start()

    def summing(m, k, j):
        return remote(pres.at[m, k], sums.at[m, k], ssend.at[m, k], srecv.at[m, k], expert=first + j)

    def sharing(m, k, j):
        mine = hidden.at[m, :, share(g)]
        return remote(mine, mine, hsend.at[m, k], hrecv.at[m, k], expert=first + j)

    own_up.wait()
    for copy in ups:
        copy.wait_recv()
    for m in range(batches):
        own_rows[m].wait()
        each(1, n, lambda k, m=m: dispatch(m, k).wait_recv())
        for k, j in peers:
            pres[m, k] = jnp.dot(x[m], up_all[j], preferred_element_type=F32).astype(BF16)
            summing(m, k, j).start()
        if m == 0:
            for copy in downs:
                copy.start()
        own_pre[...] = jnp.dot(x[m], up_all[g], preferred_element_type=F32)
        for k, j in peers:
            summing(m, k, j).wait_recv()
        total = own_pre[...]
        for k in range(1, GROUP):
            total = total + sums[m, k].astype(F32)
        hidden[m, :, share(g)] = jax.nn.silu(total).astype(BF16)
        for k, j in peers:
            sharing(m, k, j).start()

    def give(m, target):
        return remote(
            out.at[m, rows_of(target), :], ret.at[m, me], rsend.at[m, target], rrecv.at[m, me],
            pipe=ahead, expert=target,
        )

    own_down.wait()
    for copy in downs:
        copy.wait_recv()
    for m in range(batches):
        for k, j in peers:
            sharing(m, k, j).wait_recv()

        def block(index, m=m):
            owner = (group_index + 1 + index) % blocks
            rows = pl.ds(pl.multiple_of(owner * tall, 16), tall)
            out[m, rows, :] = jnp.dot(
                hidden[m, rows, :], down_all[...], preferred_element_type=F32
            ).astype(BF16)
            for j in range(GROUP):
                give(m, owner * GROUP + j).start()

        each(0, blocks, block)

    for copy in ups + downs:
        copy.wait_send()
    for copy in shifts:
        copy.wait()
    for m in range(batches):
        each(1, n, lambda k, m=m: dispatch(m, k).wait_send())
        for k, j in peers:
            summing(m, k, j).wait_send()
            sharing(m, k, j).wait_send()

        def finish(source, m=m):
            give(m, source).wait_send()
            remote(
                out.at[m, rows_of(source), :], ret.at[m, source], rsend.at[m, source],
                rrecv.at[m, source], pipe=ahead, expert=source,
            ).wait_recv()

        each(0, n, finish)


def local(pipes, activations, expert_ids, gate_values, norm_gain, up_weight, down_weight):
    n = lax.axis_size("expert")
    experts = n // GROUP
    _, batches, tok, width = activations.shape
    part = width // GROUP
    units = up_weight.shape[2]
    capacity = max(2, 3 * tok // (2 * experts))
    capacity = (capacity + 15) // 16 * 16
    rows = n * capacity

    onehot = (expert_ids[0][..., None] == jnp.arange(experts, dtype=jnp.int32)).astype(jnp.int32)
    ranking = jnp.sum((jnp.cumsum(onehot, axis=1) - onehot) * onehot, axis=-1)
    slot = expert_ids[0] * capacity + ranking
    slots = jnp.arange(experts * capacity, dtype=jnp.int32).reshape(1, experts, capacity, 1)
    place = (slot[:, None, None, :] == slots).astype(BF16)

    vmem, far = pl.BlockSpec(memory_space=pltpu.VMEM), pl.BlockSpec(memory_space=pl.ANY)
    shape, sem = jax.ShapeDtypeStruct, pltpu.SemaphoreType.DMA
    returned, act_prev, place_prev, gate_prev = pl.pallas_call(
        functools.partial(layer_kernel, n, pipes),
        out_shape=(
            shape((batches, n, capacity, part), BF16),
            shape((batches, tok, width), BF16),
            shape(place.shape, BF16),
            shape((batches, tok), F32),
        ),
        in_specs=[vmem] * 4 + [far] * 2,
        out_specs=(far,) * 4,
        scratch_shapes=[
            pltpu.VMEM((batches, n, capacity, part), BF16),
            pltpu.VMEM((batches, rows, part), BF16),
            pltpu.VMEM((GROUP, part, units), BF16),
            pltpu.VMEM((GROUP * units, part), BF16),
            pltpu.VMEM((batches, GROUP, rows, units), BF16),
            pltpu.VMEM((batches, GROUP, rows, units), BF16),
            pltpu.VMEM((rows, units), F32),
            pltpu.VMEM((batches, rows, GROUP * units), BF16),
            pltpu.VMEM((batches, rows, part), BF16),
            sem((GROUP,)),
            sem((GROUP,)),
            sem((GROUP,)),
            sem((GROUP,)),
            sem((3,)),
            sem((3,)),
            sem((batches, n)),
            sem((batches, n)),
            sem((batches, GROUP)),
            sem((batches, GROUP)),
            sem((batches, GROUP)),
            sem((batches, GROUP)),
            sem((batches, n)),
            sem((batches, n)),
            sem((2 + batches,)),
        ],
        compiler_params=pltpu.CompilerParams(
            collective_id=0, has_side_effects=True, vmem_limit_bytes=60 * 2**20
        ),
    )(
        place,
        activations[0],
        norm_gain,
        gate_values[0],
        up_weight[0].reshape(GROUP, part, units),
        down_weight[0],
    )

    returned = returned.reshape(batches, experts, GROUP, capacity, part)
    finished = []
    for m in range(batches):
        table = returned[m].transpose(0, 2, 1, 3).reshape(experts * capacity, width)
        expert_out = lax.dot_general(
            place_prev[m].reshape(experts * capacity, tok),
            table,
            (((0,), (0,)), ((), ())),
            preferred_element_type=F32,
        )
        finished.append((act_prev[m].astype(F32) + gate_prev[m][:, None] * expert_out).astype(BF16))
    return jnp.stack(finished)[None]


def solution(mesh):
    placed = (
        P("pipe", None, "expert", None),
        P("pipe", None, "expert"),
        P("pipe", None, "expert"),
        P("pipe", None),
        P("pipe", None, "expert"),
        P("pipe", "expert", None),
    )
    return jax.shard_map(
        functools.partial(local, mesh.shape["pipe"]),
        mesh=mesh,
        in_specs=placed,
        out_specs=P("pipe", None, "expert", None),
        check_vma=False,
    )
```

```python
import functools

import jax
import jax.numpy as jnp
from jax import lax
from jax.experimental import pallas as pl
from jax.experimental.pallas import tpu as pltpu
from jax.sharding import PartitionSpec as P

LEVELS = 2


EPSILON = 1e-06
GROUP = 2**LEVELS
MESH = pl.DeviceIdType.MESH
F32, BF16 = jnp.float32, jnp.bfloat16


def remote(source, target, send, recv, **where):
    return pltpu.make_async_remote_copy(
        src_ref=source, dst_ref=target, send_sem=send, recv_sem=recv, device_id=where, device_id_type=MESH
    )


def each(low, high, body):
    def step(index, carry):
        body(index)
        return carry

    lax.fori_loop(low, high, step, 0)


def layer_kernel(
    n, pipes, place, act, gain, gate, up, down, ret, act_out, place_out, gate_out,
    packed, x, up_all, down_all, pres, sums, own_pre, hidden, out,
    usend, urecv, dsend, drecv, psend, precv, xsend, xrecv, ssend, srecv, hsend, hrecv, rsend, rrecv, own,
):
    me, pipe = lax.axis_index("expert"), lax.axis_index("pipe")
    group_index = me // GROUP
    first = group_index * GROUP
    g = me - first
    batches, experts, capacity = place.shape[:3]
    part, units = up.shape[1:]
    ahead, behind = (pipe + 1) % pipes, (pipe + pipes - 1) % pipes
    blocks = n // GROUP
    tall = GROUP * capacity

    barrier = pltpu.get_barrier_semaphore()

    def greet(k):
        pl.semaphore_signal(barrier, inc=1, device_id={"expert": (me + k) % n}, device_id_type=MESH)

    def greet_behind(k):
        pl.semaphore_signal(barrier, inc=1, device_id={"pipe": behind, "expert": k}, device_id_type=MESH)

    each(1, n, greet)
    each(0, n, greet_behind)
    pl.semaphore_wait(barrier, 2 * n - 1)

    def columns(j):
        return pl.ds(pl.multiple_of(j * part, 128), part)

    def share(j):
        return pl.ds(pl.multiple_of(j * units, 128), units)

    def rows_of(d):
        return pl.ds(pl.multiple_of(d * capacity, 16), capacity)

    peers = [(k, (g + k) % GROUP) for k in range(1, GROUP)]
    ups = [remote(up.at[j], up_all.at[g], usend.at[k], urecv.at[k], expert=first + j) for k, j in peers]
    downs = [
        remote(
            down.at[:, columns(j)], down_all.at[share(g), :], dsend.at[k], drecv.at[k], expert=first + j
        )
        for k, j in peers
    ]
    shifts = [
        remote(source, target, psend.at[i], precv.at[i], pipe=ahead)
        for i, (source, target) in enumerate(((act, act_out), (place, place_out), (gate, gate_out)))
    ]

    def dispatch(m, k):
        d = (me + k) % n
        return remote(packed.at[m, d], x.at[m, rows_of(me), :], xsend.at[m, k], xrecv.at[m, k], expert=d)

    for copy in ups:
        copy.start()
    own_up = pltpu.make_async_copy(up.at[g], up_all.at[g], own.at[0])
    own_down = pltpu.make_async_copy(down.at[:, columns(g)], down_all.at[share(g), :], own.at[1])
    own_up.start()
    own_down.start()
    own_rows = []
    for m in range(batches):
        wide = act[m].astype(F32)
        scale = lax.rsqrt(jnp.mean(wide * wide, axis=-1, keepdims=True) + EPSILON)
        normed = (wide * scale * gain[...].astype(F32)).astype(BF16)
        for e in range(experts):
            for j in range(GROUP):
                packed[m, e * GROUP + j] = jnp.dot(
                    place[m, e], normed[:, j * part : (j + 1) * part], preferred_element_type=F32
                ).astype(BF16)
        if m == 0:
            each(1, n, lambda k: dispatch(0, k).start())
        copy = pltpu.make_async_copy(packed.at[m, me], x.at[m, rows_of(me), :], own.at[2 + m])
        copy.start()
        own_rows.append(copy)

    def summing(m, k, j):
        return remote(pres.at[m, k], sums.at[m, k], ssend.at[m, k], srecv.at[m, k], expert=first + j)

    def sharing(m, k, j):
        mine = hidden.at[m, :, share(g)]
        return remote(mine, mine, hsend.at[m, k], hrecv.at[m, k], expert=first + j)

    own_up.wait()
    for copy in ups:
        copy.wait_recv()
    for m in range(batches):
        own_rows[m].wait()
        each(1, n, lambda k, m=m: dispatch(m, k).wait_recv())
        for k, j in peers:
            pres[m, k] = jnp.dot(x[m], up_all[j], preferred_element_type=F32).astype(BF16)
            summing(m, k, j).start()
        if m + 1 < batches:
            each(1, n, lambda k, m=m: dispatch(m + 1, k).start())
        if m == 0:
            for copy in downs + shifts:
                copy.start()
        own_pre[...] = jnp.dot(x[m], up_all[g], preferred_element_type=F32)
        for k, j in peers:
            summing(m, k, j).wait_recv()
        total = own_pre[...]
        for k in range(1, GROUP):
            total = total + sums[m, k].astype(F32)
        hidden[m, :, share(g)] = jax.nn.silu(total).astype(BF16)
        for k, j in peers:
            sharing(m, k, j).start()

    def slots_of(m, source):
        return ret.at[m, rows_of(source // GROUP), columns(source % GROUP)]

    def give(m, target):
        return remote(
            out.at[m, rows_of(target), :], slots_of(m, me), rsend.at[m, target], rrecv.at[m, me],
            pipe=ahead, expert=target,
        )

    own_down.wait()
    for copy in downs:
        copy.wait_recv()
    for m in range(batches):
        for k, j in peers:
            sharing(m, k, j).wait_recv()

        def block(index, m=m):
            owner = (group_index + 1 + index) % blocks
            rows = pl.ds(pl.multiple_of(owner * tall, 16), tall)
            out[m, rows, :] = jnp.dot(
                hidden[m, rows, :], down_all[...], preferred_element_type=F32
            ).astype(BF16)
            for j in range(GROUP):
                give(m, owner * GROUP + j).start()

        each(0, blocks, block)

    for copy in ups + downs:
        copy.wait_send()
    for copy in shifts:
        copy.wait()
    for m in range(batches):
        each(1, n, lambda k, m=m: dispatch(m, k).wait_send())
        for k, j in peers:
            summing(m, k, j).wait_send()
            sharing(m, k, j).wait_send()

        def finish(source, m=m):
            give(m, source).wait_send()
            remote(
                out.at[m, rows_of(source), :], slots_of(m, source), rsend.at[m, source],
                rrecv.at[m, source], pipe=ahead, expert=source,
            ).wait_recv()

        each(0, n, finish)


def local(pipes, activations, expert_ids, gate_values, norm_gain, up_weight, down_weight):
    n = lax.axis_size("expert")
    experts = n // GROUP
    _, batches, tok, width = activations.shape
    part = width // GROUP
    units = up_weight.shape[2]
    capacity = max(2, 3 * tok // (2 * experts))
    capacity = (capacity + 15) // 16 * 16
    rows = n * capacity

    onehot = (expert_ids[0][..., None] == jnp.arange(experts, dtype=jnp.int32)).astype(jnp.int32)
    ranking = jnp.sum((jnp.cumsum(onehot, axis=1) - onehot) * onehot, axis=-1)
    slot = expert_ids[0] * capacity + ranking
    slots = jnp.arange(experts * capacity, dtype=jnp.int32).reshape(1, experts, capacity, 1)
    place = (slot[:, None, None, :] == slots).astype(BF16)

    vmem, far = pl.BlockSpec(memory_space=pltpu.VMEM), pl.BlockSpec(memory_space=pl.ANY)
    shape, sem = jax.ShapeDtypeStruct, pltpu.SemaphoreType.DMA
    returned, act_prev, place_prev, gate_prev = pl.pallas_call(
        functools.partial(layer_kernel, n, pipes),
        out_shape=(
            shape((batches, experts * capacity, width), BF16),
            shape((batches, tok, width), BF16),
            shape(place.shape, BF16),
            shape((batches, tok), F32),
        ),
        in_specs=[vmem] * 4 + [far] * 2,
        out_specs=(far,) * 4,
        scratch_shapes=[
            pltpu.VMEM((batches, n, capacity, part), BF16),
            pltpu.VMEM((batches, rows, part), BF16),
            pltpu.VMEM((GROUP, part, units), BF16),
            pltpu.VMEM((GROUP * units, part), BF16),
            pltpu.VMEM((batches, GROUP, rows, units), BF16),
            pltpu.VMEM((batches, GROUP, rows, units), BF16),
            pltpu.VMEM((rows, units), F32),
            pltpu.VMEM((batches, rows, GROUP * units), BF16),
            pltpu.VMEM((batches, rows, part), BF16),
            sem((GROUP,)),
            sem((GROUP,)),
            sem((GROUP,)),
            sem((GROUP,)),
            sem((3,)),
            sem((3,)),
            sem((batches, n)),
            sem((batches, n)),
            sem((batches, GROUP)),
            sem((batches, GROUP)),
            sem((batches, GROUP)),
            sem((batches, GROUP)),
            sem((batches, n)),
            sem((batches, n)),
            sem((2 + batches,)),
        ],
        compiler_params=pltpu.CompilerParams(
            collective_id=0, has_side_effects=True, vmem_limit_bytes=60 * 2**20
        ),
    )(
        place,
        activations[0],
        norm_gain,
        gate_values[0],
        up_weight[0].reshape(GROUP, part, units),
        down_weight[0],
    )

    finished = []
    for m in range(batches):
        expert_out = lax.dot_general(
            place_prev[m].reshape(experts * capacity, tok),
            returned[m],
            (((0,), (0,)), ((), ())),
            preferred_element_type=F32,
        )
        finished.append((act_prev[m].astype(F32) + gate_prev[m][:, None] * expert_out).astype(BF16))
    return jnp.stack(finished)[None]


def solution(mesh):
    placed = (
        P("pipe", None, "expert", None),
        P("pipe", None, "expert"),
        P("pipe", None, "expert"),
        P("pipe", None),
        P("pipe", None, "expert"),
        P("pipe", "expert", None),
    )
    return jax.shard_map(
        functools.partial(local, mesh.shape["pipe"]),
        mesh=mesh,
        in_specs=placed,
        out_specs=P("pipe", None, "expert", None),
        check_vma=False,
    )
```

```python
import functools

import jax
import jax.numpy as jnp
from jax import lax
from jax.experimental import pallas as pl
from jax.experimental.pallas import tpu as pltpu
from jax.sharding import PartitionSpec as P

LEVELS = 2


EPSILON = 1e-06
GROUP = 2**LEVELS
MESH = pl.DeviceIdType.MESH
F32, BF16 = jnp.float32, jnp.bfloat16


def remote(source, target, send, recv, **where):
    return pltpu.make_async_remote_copy(
        src_ref=source, dst_ref=target, send_sem=send, recv_sem=recv, device_id=where, device_id_type=MESH
    )


def each(low, high, body):
    def step(index, carry):
        body(index)
        return carry

    lax.fori_loop(low, high, step, 0)


def layer_kernel(
    n, pipes, place, act, gain, gate, up, down, ret, act_out, place_out, gate_out,
    packed, x, up_all, down_all, pres, sums, own_pre, hidden, out,
    usend, urecv, dsend, drecv, psend, precv, xsend, xrecv, ssend, srecv, hsend, hrecv, rsend, rrecv, own,
):
    me, pipe = lax.axis_index("expert"), lax.axis_index("pipe")
    group_index = me // GROUP
    first = group_index * GROUP
    g = me - first
    batches, experts, capacity = place.shape[:3]
    part, units = up.shape[1:]
    ahead, behind = (pipe + 1) % pipes, (pipe + pipes - 1) % pipes
    blocks = n // GROUP
    tall = GROUP * capacity

    barrier = pltpu.get_barrier_semaphore()

    def greet(k):
        pl.semaphore_signal(barrier, inc=1, device_id={"expert": (me + k) % n}, device_id_type=MESH)

    def greet_behind(k):
        pl.semaphore_signal(barrier, inc=1, device_id={"pipe": behind, "expert": k}, device_id_type=MESH)

    each(1, n, greet)
    each(0, n, greet_behind)
    pl.semaphore_wait(barrier, 2 * n - 1)

    def columns(j):
        return pl.ds(pl.multiple_of(j * part, 128), part)

    def share(j):
        return pl.ds(pl.multiple_of(j * units, 128), units)

    def rows_of(d):
        return pl.ds(pl.multiple_of(d * capacity, 16), capacity)

    peers = [(k, (g + k) % GROUP) for k in range(1, GROUP)]
    ups = [remote(up.at[j], up_all.at[g], usend.at[k], urecv.at[k], expert=first + j) for k, j in peers]
    downs = [
        remote(
            down.at[:, columns(j)], down_all.at[share(g), :], dsend.at[k], drecv.at[k], expert=first + j
        )
        for k, j in peers
    ]
    shifts = [
        remote(source, target, psend.at[i], precv.at[i], pipe=ahead)
        for i, (source, target) in enumerate(((act, act_out), (place, place_out), (gate, gate_out)))
    ]

    def dispatch(m, k):
        d = (me + k) % n
        return remote(packed.at[m, d], x.at[m, rows_of(me), :], xsend.at[m, k], xrecv.at[m, k], expert=d)

    for copy in ups:
        copy.start()
    own_up = pltpu.make_async_copy(up.at[g], up_all.at[g], own.at[0])
    own_down = pltpu.make_async_copy(down.at[:, columns(g)], down_all.at[share(g), :], own.at[1])
    own_up.start()
    own_down.start()
    own_rows = []
    for m in range(batches):
        wide = act[m].astype(F32)
        scale = lax.rsqrt(jnp.mean(wide * wide, axis=-1, keepdims=True) + EPSILON)
        normed = (wide * scale * gain[...].astype(F32)).astype(BF16)
        for e in range(experts):
            for j in range(GROUP):
                packed[m, e * GROUP + j] = jnp.dot(
                    place[m, e], normed[:, j * part : (j + 1) * part], preferred_element_type=F32
                ).astype(BF16)
        if m == 0:
            each(1, n, lambda k: dispatch(0, k).start())
        copy = pltpu.make_async_copy(packed.at[m, me], x.at[m, rows_of(me), :], own.at[2 + m])
        copy.start()
        own_rows.append(copy)

    def summing(m, k, j):
        return remote(pres.at[m, k], sums.at[m, k], ssend.at[m, k], srecv.at[m, k], expert=first + j)

    def sharing(m, k, j):
        mine = hidden.at[m, :, share(g)]
        return remote(mine, mine, hsend.at[m, k], hrecv.at[m, k], expert=first + j)

    def slots_of(m, source):
        return ret.at[m, rows_of(source // GROUP), columns(source % GROUP)]

    def give(m, target):
        return remote(
            out.at[m, rows_of(target), :], slots_of(m, me), rsend.at[m, target], rrecv.at[m, me],
            pipe=ahead, expert=target,
        )

    own_up.wait()
    for copy in ups:
        copy.wait_recv()
    for m in range(batches):
        own_rows[m].wait()
        each(1, n, lambda k, m=m: dispatch(m, k).wait_recv())
        for k, j in peers:
            pres[m, k] = jnp.dot(x[m], up_all[j], preferred_element_type=F32).astype(BF16)
            summing(m, k, j).start()
        if m == 0:
            for copy in downs:
                copy.start()
        own_pre[...] = jnp.dot(x[m], up_all[g], preferred_element_type=F32)
        for k, j in peers:
            summing(m, k, j).wait_recv()
        total = own_pre[...]
        for k in range(1, GROUP):
            total = total + sums[m, k].astype(F32)
        hidden[m, :, share(g)] = jax.nn.silu(total).astype(BF16)
        for k, j in peers:
            sharing(m, k, j).start()
        if m + 1 < batches:
            each(1, n, lambda k, m=m: dispatch(m + 1, k).start())
        if m == 0:
            for copy in shifts:
                copy.start()
            own_down.wait()
            for copy in downs:
                copy.wait_recv()
        for k, j in peers:
            sharing(m, k, j).wait_recv()

        def block(index, m=m):
            owner = (group_index + 1 + index) % blocks
            rows = pl.ds(pl.multiple_of(owner * tall, 16), tall)
            out[m, rows, :] = jnp.dot(
                hidden[m, rows, :], down_all[...], preferred_element_type=F32
            ).astype(BF16)
            for j in range(GROUP):
                give(m, owner * GROUP + j).start()

        each(0, blocks, block)

    for copy in ups + downs:
        copy.wait_send()
    for copy in shifts:
        copy.wait()
    for m in range(batches):
        each(1, n, lambda k, m=m: dispatch(m, k).wait_send())
        for k, j in peers:
            summing(m, k, j).wait_send()
            sharing(m, k, j).wait_send()

        def finish(source, m=m):
            give(m, source).wait_send()
            remote(
                out.at[m, rows_of(source), :], slots_of(m, source), rsend.at[m, source],
                rrecv.at[m, source], pipe=ahead, expert=source,
            ).wait_recv()

        each(0, n, finish)


def local(pipes, activations, expert_ids, gate_values, norm_gain, up_weight, down_weight):
    n = lax.axis_size("expert")
    experts = n // GROUP
    _, batches, tok, width = activations.shape
    part = width // GROUP
    units = up_weight.shape[2]
    capacity = max(2, 3 * tok // (2 * experts))
    capacity = (capacity + 15) // 16 * 16
    rows = n * capacity

    onehot = (expert_ids[0][..., None] == jnp.arange(experts, dtype=jnp.int32)).astype(jnp.int32)
    ranking = jnp.sum((jnp.cumsum(onehot, axis=1) - onehot) * onehot, axis=-1)
    slot = expert_ids[0] * capacity + ranking
    slots = jnp.arange(experts * capacity, dtype=jnp.int32).reshape(1, experts, capacity, 1)
    place = (slot[:, None, None, :] == slots).astype(BF16)

    vmem, far = pl.BlockSpec(memory_space=pltpu.VMEM), pl.BlockSpec(memory_space=pl.ANY)
    shape, sem = jax.ShapeDtypeStruct, pltpu.SemaphoreType.DMA
    returned, act_prev, place_prev, gate_prev = pl.pallas_call(
        functools.partial(layer_kernel, n, pipes),
        out_shape=(
            shape((batches, experts * capacity, width), BF16),
            shape((batches, tok, width), BF16),
            shape(place.shape, BF16),
            shape((batches, tok), F32),
        ),
        in_specs=[vmem] * 4 + [far] * 2,
        out_specs=(far,) * 4,
        scratch_shapes=[
            pltpu.VMEM((batches, n, capacity, part), BF16),
            pltpu.VMEM((batches, rows, part), BF16),
            pltpu.VMEM((GROUP, part, units), BF16),
            pltpu.VMEM((GROUP * units, part), BF16),
            pltpu.VMEM((batches, GROUP, rows, units), BF16),
            pltpu.VMEM((batches, GROUP, rows, units), BF16),
            pltpu.VMEM((rows, units), F32),
            pltpu.VMEM((batches, rows, GROUP * units), BF16),
            pltpu.VMEM((batches, rows, part), BF16),
            sem((GROUP,)),
            sem((GROUP,)),
            sem((GROUP,)),
            sem((GROUP,)),
            sem((3,)),
            sem((3,)),
            sem((batches, n)),
            sem((batches, n)),
            sem((batches, GROUP)),
            sem((batches, GROUP)),
            sem((batches, GROUP)),
            sem((batches, GROUP)),
            sem((batches, n)),
            sem((batches, n)),
            sem((2 + batches,)),
        ],
        compiler_params=pltpu.CompilerParams(
            collective_id=0, has_side_effects=True, vmem_limit_bytes=60 * 2**20
        ),
    )(
        place,
        activations[0],
        norm_gain,
        gate_values[0],
        up_weight[0].reshape(GROUP, part, units),
        down_weight[0],
    )

    finished = []
    for m in range(batches):
        expert_out = lax.dot_general(
            place_prev[m].reshape(experts * capacity, tok),
            returned[m],
            (((0,), (0,)), ((), ())),
            preferred_element_type=F32,
        )
        finished.append((act_prev[m].astype(F32) + gate_prev[m][:, None] * expert_out).astype(BF16))
    return jnp.stack(finished)[None]


def solution(mesh):
    placed = (
        P("pipe", None, "expert", None),
        P("pipe", None, "expert"),
        P("pipe", None, "expert"),
        P("pipe", None),
        P("pipe", None, "expert"),
        P("pipe", "expert", None),
    )
    return jax.shard_map(
        functools.partial(local, mesh.shape["pipe"]),
        mesh=mesh,
        in_specs=placed,
        out_specs=P("pipe", None, "expert", None),
        check_vma=False,
    )
```

```python
import functools

import jax
import jax.numpy as jnp
from jax import lax
from jax.experimental import pallas as pl
from jax.experimental.pallas import tpu as pltpu
from jax.sharding import PartitionSpec as P

LEVELS = 2


EPSILON = 1e-06
GROUP = 2**LEVELS
MESH = pl.DeviceIdType.MESH
F32, BF16 = jnp.float32, jnp.bfloat16


def remote(source, target, send, recv, **where):
    return pltpu.make_async_remote_copy(
        src_ref=source, dst_ref=target, send_sem=send, recv_sem=recv, device_id=where, device_id_type=MESH
    )


def each(low, high, body):
    def step(index, carry):
        body(index)
        return carry

    lax.fori_loop(low, high, step, 0)


def layer_kernel(
    n, pipes, place, act, gain, gate, up, down, ret, act_out, place_out, gate_out,
    packed, x, up_all, down_all, pres, sums, own_pre, hidden, out,
    usend, urecv, dsend, drecv, psend, precv, xsend, xrecv, ssend, srecv, hsend, hrecv, rsend, rrecv, own,
):
    me, pipe = lax.axis_index("expert"), lax.axis_index("pipe")
    group_index = me // GROUP
    first = group_index * GROUP
    g = me - first
    batches, experts, capacity = place.shape[:3]
    part, units = up.shape[1:]
    ahead, behind = (pipe + 1) % pipes, (pipe + pipes - 1) % pipes
    blocks = n // GROUP
    tall = GROUP * capacity

    barrier = pltpu.get_barrier_semaphore()

    def greet(k):
        pl.semaphore_signal(barrier, inc=1, device_id={"expert": (me + k) % n}, device_id_type=MESH)

    def greet_behind(k):
        pl.semaphore_signal(barrier, inc=1, device_id={"pipe": behind, "expert": k}, device_id_type=MESH)

    each(1, n, greet)
    each(0, n, greet_behind)
    pl.semaphore_wait(barrier, 2 * n - 1)

    def columns(j):
        return pl.ds(pl.multiple_of(j * part, 128), part)

    def share(j):
        return pl.ds(pl.multiple_of(j * units, 128), units)

    def rows_of(d):
        return pl.ds(pl.multiple_of(d * capacity, 16), capacity)

    peers = [(k, (g + k) % GROUP) for k in range(1, GROUP)]
    ups = [remote(up.at[j], up_all.at[g], usend.at[k], urecv.at[k], expert=first + j) for k, j in peers]
    downs = [
        remote(
            down.at[:, columns(j)], down_all.at[share(g), :], dsend.at[k], drecv.at[k], expert=first + j
        )
        for k, j in peers
    ]
    shifts = [
        remote(source, target, psend.at[i], precv.at[i], pipe=ahead)
        for i, (source, target) in enumerate(((act, act_out), (place, place_out), (gate, gate_out)))
    ]

    def dispatch(m, k):
        d = (me + k) % n
        return remote(packed.at[m, d], x.at[m, rows_of(me), :], xsend.at[m, k], xrecv.at[m, k], expert=d)

    for copy in ups:
        copy.start()
    own_up = pltpu.make_async_copy(up.at[g], up_all.at[g], own.at[0])
    own_down = pltpu.make_async_copy(down.at[:, columns(g)], down_all.at[share(g), :], own.at[1])
    own_up.start()
    own_down.start()
    own_rows = []
    for m in range(batches):
        wide = act[m].astype(F32)
        scale = lax.rsqrt(jnp.mean(wide * wide, axis=-1, keepdims=True) + EPSILON)
        normed = (wide * scale * gain[...].astype(F32)).astype(BF16)
        for e in range(experts):
            for j in range(GROUP):
                packed[m, e * GROUP + j] = jnp.dot(
                    place[m, e], normed[:, j * part : (j + 1) * part], preferred_element_type=F32
                ).astype(BF16)
        if m == 0:
            each(1, n, lambda k: dispatch(0, k).start())
            for copy in downs:
                copy.start()
        copy = pltpu.make_async_copy(packed.at[m, me], x.at[m, rows_of(me), :], own.at[2 + m])
        copy.start()
        own_rows.append(copy)

    def summing(m, k, j):
        return remote(pres.at[m, k], sums.at[m, k], ssend.at[m, k], srecv.at[m, k], expert=first + j)

    def sharing(m, k, j):
        mine = hidden.at[m, :, share(g)]
        return remote(mine, mine, hsend.at[m, k], hrecv.at[m, k], expert=first + j)

    def slots_of(m, source):
        return ret.at[m, rows_of(source // GROUP), columns(source % GROUP)]

    def give(m, target):
        return remote(
            out.at[m, rows_of(target), :], slots_of(m, me), rsend.at[m, target], rrecv.at[m, me],
            pipe=ahead, expert=target,
        )

    own_up.wait()
    for copy in ups:
        copy.wait_recv()
    for m in range(batches):
        own_rows[m].wait()
        each(1, n, lambda k, m=m: dispatch(m, k).wait_recv())
        for k, j in peers:
            pres[m, k] = jnp.dot(x[m], up_all[j], preferred_element_type=F32).astype(BF16)
            summing(m, k, j).start()
        if m + 1 < batches:
            each(1, n, lambda k, m=m: dispatch(m + 1, k).start())
        own_pre[...] = jnp.dot(x[m], up_all[g], preferred_element_type=F32)
        for k, j in peers:
            summing(m, k, j).wait_recv()
        total = own_pre[...]
        for k in range(1, GROUP):
            total = total + sums[m, k].astype(F32)
        hidden[m, :, share(g)] = jax.nn.silu(total).astype(BF16)
        for k, j in peers:
            sharing(m, k, j).start()
        if m == 0:
            for copy in shifts:
                copy.start()
            own_down.wait()
            for copy in downs:
                copy.wait_recv()
        for k, j in peers:
            sharing(m, k, j).wait_recv()

        def block(index, m=m):
            owner = (group_index + 1 + index) % blocks
            rows = pl.ds(pl.multiple_of(owner * tall, 16), tall)
            out[m, rows, :] = jnp.dot(
                hidden[m, rows, :], down_all[...], preferred_element_type=F32
            ).astype(BF16)
            for j in range(GROUP):
                give(m, owner * GROUP + j).start()

        each(0, blocks, block)

    for copy in ups + downs:
        copy.wait_send()
    for copy in shifts:
        copy.wait()
    for m in range(batches):
        each(1, n, lambda k, m=m: dispatch(m, k).wait_send())
        for k, j in peers:
            summing(m, k, j).wait_send()
            sharing(m, k, j).wait_send()

        def finish(source, m=m):
            give(m, source).wait_send()
            remote(
                out.at[m, rows_of(source), :], slots_of(m, source), rsend.at[m, source],
                rrecv.at[m, source], pipe=ahead, expert=source,
            ).wait_recv()

        each(0, n, finish)


def local(pipes, activations, expert_ids, gate_values, norm_gain, up_weight, down_weight):
    n = lax.axis_size("expert")
    experts = n // GROUP
    _, batches, tok, width = activations.shape
    part = width // GROUP
    units = up_weight.shape[2]
    capacity = max(2, 3 * tok // (2 * experts))
    capacity = (capacity + 15) // 16 * 16
    rows = n * capacity

    onehot = (expert_ids[0][..., None] == jnp.arange(experts, dtype=jnp.int32)).astype(jnp.int32)
    ranking = jnp.sum((jnp.cumsum(onehot, axis=1) - onehot) * onehot, axis=-1)
    slot = expert_ids[0] * capacity + ranking
    slots = jnp.arange(experts * capacity, dtype=jnp.int32).reshape(1, experts, capacity, 1)
    place = (slot[:, None, None, :] == slots).astype(BF16)

    vmem, far = pl.BlockSpec(memory_space=pltpu.VMEM), pl.BlockSpec(memory_space=pl.ANY)
    shape, sem = jax.ShapeDtypeStruct, pltpu.SemaphoreType.DMA
    returned, act_prev, place_prev, gate_prev = pl.pallas_call(
        functools.partial(layer_kernel, n, pipes),
        out_shape=(
            shape((batches, experts * capacity, width), BF16),
            shape((batches, tok, width), BF16),
            shape(place.shape, BF16),
            shape((batches, tok), F32),
        ),
        in_specs=[vmem] * 4 + [far] * 2,
        out_specs=(far,) * 4,
        scratch_shapes=[
            pltpu.VMEM((batches, n, capacity, part), BF16),
            pltpu.VMEM((batches, rows, part), BF16),
            pltpu.VMEM((GROUP, part, units), BF16),
            pltpu.VMEM((GROUP * units, part), BF16),
            pltpu.VMEM((batches, GROUP, rows, units), BF16),
            pltpu.VMEM((batches, GROUP, rows, units), BF16),
            pltpu.VMEM((rows, units), F32),
            pltpu.VMEM((batches, rows, GROUP * units), BF16),
            pltpu.VMEM((batches, rows, part), BF16),
            sem((GROUP,)),
            sem((GROUP,)),
            sem((GROUP,)),
            sem((GROUP,)),
            sem((3,)),
            sem((3,)),
            sem((batches, n)),
            sem((batches, n)),
            sem((batches, GROUP)),
            sem((batches, GROUP)),
            sem((batches, GROUP)),
            sem((batches, GROUP)),
            sem((batches, n)),
            sem((batches, n)),
            sem((2 + batches,)),
        ],
        compiler_params=pltpu.CompilerParams(
            collective_id=0, has_side_effects=True, vmem_limit_bytes=60 * 2**20
        ),
    )(
        place,
        activations[0],
        norm_gain,
        gate_values[0],
        up_weight[0].reshape(GROUP, part, units),
        down_weight[0],
    )

    finished = []
    for m in range(batches):
        expert_out = lax.dot_general(
            place_prev[m].reshape(experts * capacity, tok),
            returned[m],
            (((0,), (0,)), ((), ())),
            preferred_element_type=F32,
        )
        finished.append((act_prev[m].astype(F32) + gate_prev[m][:, None] * expert_out).astype(BF16))
    return jnp.stack(finished)[None]


def solution(mesh):
    placed = (
        P("pipe", None, "expert", None),
        P("pipe", None, "expert"),
        P("pipe", None, "expert"),
        P("pipe", None),
        P("pipe", None, "expert"),
        P("pipe", "expert", None),
    )
    return jax.shard_map(
        functools.partial(local, mesh.shape["pipe"]),
        mesh=mesh,
        in_specs=placed,
        out_specs=P("pipe", None, "expert", None),
        check_vma=False,
    )
```
